32 devices in a mesh: groups: 2 (over y), qry: 4 (over x, core), ref: 4 (over z).
Axes of the slice: x: 2, y: 2, z: 4, core: 2. Of those that a mesh axis runs over, the one named last changes fastest.
Arguments:
- query_feats: bfloat16 [1024, 9, 3840], P(('groups', 'qry')), parts along dimension 0, may hold values from -6 to 6
- ref_feats: bfloat16 [256, 4, 9, 3840], P(('groups', 'ref'), 'qry'), parts along dimension 0, may hold values from -6 to 6
- pair_table: int32 [8, 4], P('groups'), parts along dimension 0, may hold values from 0 to 1, as said below
- lengths: int32 [4], P('groups'), parts along dimension 0, may hold values from 1 to 96, 128 in all
- query_len: int32 [2], P('groups'), parts along dimension 0, may hold values from 64 to 128
- conv1_weight: float32 [3, 3, 32], replicated, may hold values from -2 to 2
- conv1_bias: float32 [32], replicated, may hold values from -3 to 3
- conv2_weight: bfloat16 [3, 3, 64, 32], replicated, may hold values from -0.375 to 0.375
- conv2_bias: float32 [64], replicated, may hold values from -3 to 3
- conv3_weight: bfloat16 [3, 3, 128, 64], replicated, may hold values from -0.25 to 0.25
- conv3_bias: float32 [128], replicated, may hold values from -3 to 3
- conv4_weight: bfloat16 [128], replicated, may hold values from -0.5 to 0.5
- conv4_bias: float32 [1], replicated, may hold values from -3 to 3
Outputs:
- score_map: float32 [256, 128], P(('groups', 'qry'), 'ref'), parts along dimension 0
- video_scores: float32 [4], P('groups'), parts along dimension 0
The draws below stay inside these ranges and needn't reach their ends.
There are 2 independent parts, one for each index of `groups`. The reference program is written for one: setup_inputs(seed, part) draws one part's arguments, and reference() takes and returns one part's arrays. A program takes and returns all parts, laid end to end along the dimension named above; an argument that names none is the same for every part. Nothing has to cross between parts.
Inputs may be any that keep to these rules, and one draw needn't show every extreme that they name: `pair_table`: in each row, at most 1 of the 1 tiles in the block of one index of ref are 1, and some such block holds exactly 1 in every draw.
All inputs are finite; a program needn't handle non-finite values.
Results may differ from the reference program's by a relative error of at most 0.01.
Values may be sent and summed in bfloat16 or wider, within the bound.
A program may use at most 128 MiB of HBM per device.

```python
import math
import jax
import jax.numpy as jnp
import numpy as np
from jax import lax

D = 3840
REGIONS = 9
FT = 128
C1 = 32
C2 = 64
C3 = 128
MOST = 1
RTD = 1
QT = 4
RT = 4
NQ = 512
NR = 512
VIDEOS = 2
N_REF = 4


def draw_pair_table(key, part):
    subkeys = jax.random.split(jax.random.fold_in(key, 17), 4)
    counts = jax.random.randint(subkeys[0], (QT, N_REF), 0, MOST + 1)
    pick_row = jax.random.randint(subkeys[1], (), 0, QT)
    pick_col = jax.random.randint(subkeys[2], (), 0, N_REF)
    forced = (jnp.arange(QT)[:, None] == pick_row) & (jnp.arange(N_REF)[None, :] == pick_col)
    counts = jnp.where(forced, MOST, counts)
    scores = jax.random.randint(subkeys[3], (QT, N_REF, RTD), 0, 1 << 20) * RTD + jnp.arange(RTD)
    ordering = jnp.argsort(scores, axis=-1, stable=True)
    placing = jnp.argsort(ordering, axis=-1, stable=True)
    return (placing < counts[..., None]).astype(jnp.int32).reshape(QT, RT)


def block_levels(own_key, shape, cuts, least, high):
    def one(axis_at, shards_of):
        heights = jax.random.uniform(jax.random.fold_in(jax.random.fold_in(own_key, 6), axis_at), (shards_of,), jnp.float32, least / len(cuts), high / len(cuts))
        return jnp.repeat(jnp.exp(heights), shape[axis_at] // shards_of).reshape((-1,) + (1,) * (len(shape) - axis_at - 1))

    level = one(*cuts[0])
    for cut in cuts[1:]:
        level = level * one(*cut)
    return level


def split_up(number_of, total, bound, slope):
    loads = [(1 << 20) // math.isqrt(standing ** slope) + 1 for standing in range(2, number_of + 1)]
    spare, holding = total - bound - (number_of - 1), [1] * (number_of - 1)
    while spare > 0:
        movable = [i for i in range(number_of - 1) if holding[i] < bound]
        pool, left = sum([loads[i] for i in movable]), spare
        for i in movable:
            addition = min(bound - holding[i], max(1, left * loads[i] // pool), spare)
            holding[i] = holding[i] + addition
            spare = spare - addition
    return np.array([bound] + holding)


def uneven_parts(key, number_of, total, most, slope):
    if number_of == 2:
        one = jax.random.randint(key, (), max(1, total - most), min(most, total - 1) + 1)
        return jnp.stack([one, total - one])
    sizes = jnp.asarray(split_up(number_of, total, most, slope), jnp.int32)
    pairs = (number_of - 1) // 2
    giver, receiver = sizes[1:1 + 2 * pairs:2], sizes[2:2 + 2 * pairs:2]
    slack = jnp.minimum(giver - 1, most - receiver)
    moved = jax.random.randint(jax.random.fold_in(key, 1), (pairs,), 0, 1 << 20) % (slack + 1)
    sizes = sizes.at[1:1 + 2 * pairs:2].set(giver - moved).at[2:2 + 2 * pairs:2].set(receiver + moved)
    return sizes[jax.random.permutation(jax.random.fold_in(key, 2), number_of)]


def gaussian(own_key, shape, scale, most, shards=(), kind=jnp.bfloat16):
    entries = jax.random.normal(own_key, shape, jnp.float32) * scale
    if len(shards) > 0:
        entries = block_levels(own_key, shape, shards, -0.22, 0.18) * entries
    return jnp.clip(entries, min=-most, max=most).astype(kind)


def setup_inputs(seed: int = 0, part: int = 0) -> dict:
    streams_of = jax.random.split(jax.random.key(seed), 14)
    own_keys = jax.random.split(jax.random.fold_in(streams_of[13], part), 14)
    return {
        "query_feats": gaussian(own_keys[0], (NQ, REGIONS, D), 1.0, 6.0, ((0, 4),)),
        "ref_feats": gaussian(own_keys[1], (NR // QT, QT, REGIONS, D), 1.0, 6.0, ((0, 4), (1, 4))),
        "pair_table": draw_pair_table(jax.random.fold_in(jax.random.fold_in(streams_of[13], part), 71), part),
        "lengths": uneven_parts(own_keys[3], VIDEOS, NR // 4, 3 * FT // 4, 1).astype(jnp.int32),
        "query_len": jax.random.randint(own_keys[4], (1,), NQ // 8, NQ // 4 + 1).astype(jnp.int32),
        "conv1_weight": gaussian(streams_of[5], (3, 3, C1), 9 ** -0.5, 2.0, (), jnp.float32),
        "conv1_bias": gaussian(streams_of[6], (C1,), 0.5, 3.0, (), jnp.float32),
        "conv2_weight": gaussian(streams_of[7], (3, 3, C2, C1), (9 * C1) ** -0.5, 0.375),
        "conv2_bias": gaussian(streams_of[8], (C2,), 0.5, 3.0, (), jnp.float32),
        "conv3_weight": gaussian(streams_of[9], (3, 3, C3, C2), (9 * C2) ** -0.5, 0.25),
        "conv3_bias": gaussian(streams_of[10], (C3,), 0.5, 3.0, (), jnp.float32),
        "conv4_weight": gaussian(streams_of[11], (C3,), C3 ** -0.5, 0.5),
        "conv4_bias": gaussian(streams_of[12], (1,), 0.5, 3.0, (), jnp.float32),
    }


def slot_table(mask, most):
    width = mask.shape[-1]
    ranking = (jnp.cumsum(mask, axis=-1) - 1).astype(jnp.int32)
    slot_ids = jnp.arange(most, dtype=jnp.int32)
    chosen = (mask[..., None, :] == 1) & (ranking[..., None, :] == slot_ids[:, None])
    picked = lax.optimization_barrier(jnp.sum(jnp.where(chosen, jnp.arange(width, dtype=jnp.int32), 0), axis=-1)).astype(jnp.int32)
    return (chosen, picked)

def frame_sims(query_mat, ref_mat, regions):
    products = lax.dot_general(query_mat, ref_mat, (((1,), (1,)), ((), ())), preferred_element_type=jnp.float32, precision=lax.Precision.HIGHEST)
    frames = query_mat.shape[0] // regions
    others = ref_mat.shape[0] // regions
    best = lax.optimization_barrier(jnp.max(products.reshape(frames, regions, others, regions), axis=3))
    return lax.optimization_barrier(jnp.sum(best, axis=1)) * (1.0 / (regions * math.sqrt(query_mat.shape[1])))

def conv_layer(padded, weights, bias, block_rows, use_relu, use_pool):
    channels = padded.shape[0]
    height = padded.shape[1] - 2
    width = padded.shape[2] - 2
    block_rows = math.gcd(height, block_rows)
    outputs = weights.shape[0]

    def one_block(position):
        window = lax.dynamic_slice_in_dim(padded, position * block_rows, block_rows + 2, 1)
        stacked = jnp.concatenate([window[:, shift_row:shift_row + block_rows, shift_col:shift_col + width] for shift_row in range(3) for shift_col in range(3)], axis=0)
        result = jnp.dot(weights, stacked.reshape(9 * channels, block_rows * width), preferred_element_type=jnp.float32, precision=lax.Precision.HIGHEST)
        result = (result + bias[:, None]).reshape(outputs, block_rows, width)
        if use_relu:
            result = jnp.maximum(result, 0.0)
        if use_pool:
            result = lax.optimization_barrier(jnp.max(result.reshape(outputs, block_rows // 2, 2, width // 2, 2), axis=(2, 4)))
        return result
    blocks = lax.map(one_block, jnp.arange(height // block_rows, dtype=jnp.int32))
    return jnp.transpose(blocks, (1, 0, 2, 3)).reshape(outputs, -1, blocks.shape[-1])

def rounded(values):
    return lax.optimization_barrier(values.astype(jnp.bfloat16)).astype(jnp.float32)

def padded_map(values):
    return jnp.pad(values, ((0, 0), (1, 1), (1, 1)))

def weight_matrix(weight):
    return jnp.transpose(weight, (2, 0, 1, 3)).reshape(weight.shape[2], -1).astype(jnp.float32)

def reference(query_feats, ref_feats, pair_table, lengths, query_len, conv1_weight, conv1_bias, conv2_weight, conv2_bias, conv3_weight, conv3_bias, conv4_weight, conv4_bias):
    queries = query_feats.astype(jnp.float32).reshape(QT, FT * REGIONS, D)
    references = ref_feats.astype(jnp.float32).reshape(RT, FT * REGIONS, D)
    chosen, picked = slot_table(pair_table.reshape(QT, N_REF, RTD), MOST)

    def tile_block(position):
        qry_index = position // N_REF
        ref_index = position % N_REF
        query_mat = queries[qry_index]

        def one_slot(slot_id):
            return frame_sims(query_mat, references[ref_index * RTD + picked[qry_index, ref_index, slot_id]], REGIONS)
        sims = lax.map(one_slot, jnp.arange(MOST, dtype=jnp.int32))
        placed = jnp.einsum('st,sqf->qtf', chosen[qry_index, ref_index].astype(jnp.float32), sims, precision=lax.Precision.HIGHEST)
        return placed.reshape(FT, RTD * FT)
    blocks = lax.map(tile_block, jnp.arange(QT * N_REF, dtype=jnp.int32))
    sim_map = blocks.reshape(QT, N_REF, FT, RTD * FT).transpose(0, 2, 1, 3).reshape(1, NQ, NR)
    first_weights = conv1_weight.astype(jnp.float32).transpose(2, 0, 1).reshape(C1, 9)
    first = rounded(conv_layer(padded_map(sim_map), first_weights, conv1_bias, 32, True, True))
    second = rounded(conv_layer(padded_map(first), weight_matrix(conv2_weight), conv2_bias, 16, True, True))
    third = rounded(conv_layer(padded_map(second), weight_matrix(conv3_weight), conv3_bias, 16, True, False))
    last_weights = conv4_weight.astype(jnp.float32).reshape(1, C3)
    score_map = jnp.dot(last_weights, third.reshape(C3, -1), preferred_element_type=jnp.float32, precision=lax.Precision.HIGHEST).reshape(NQ // 4, NR // 4) + conv4_bias[0]
    ends = jnp.cumsum(lengths).astype(jnp.int32)
    starts = ends - lengths
    column = jnp.arange(NR // 4, dtype=jnp.int32)
    member = (column[:, None] >= starts[None, :]) & (column[:, None] < ends[None, :])
    peaks = lax.optimization_barrier(jnp.max(jnp.where(member[None], score_map[:, :, None], -jnp.inf), axis=1))
    row_ids = jnp.arange(NQ // 4, dtype=jnp.int32)
    totals = lax.optimization_barrier(jnp.sum(jnp.where((row_ids < query_len[0])[:, None], peaks, 0.0), axis=0))
    return (score_map, totals / query_len[0].astype(jnp.float32))
```

```python
import functools
import math

import jax
import jax.numpy as jnp
import numpy as np
from jax import lax
from jax.experimental import pallas as pl
from jax.experimental.pallas import tpu as pltpu
from jax.sharding import PartitionSpec as P

MESH = pl.DeviceIdType.MESH
HALO = 8
PITCH = 40
LEAD = 48


def sims_kernel(
    chips, regions, frames, scale, chunk, q_hbm, r_hbm, out_ref, q_buf, r_buf, acc,
    q_sem, own_sem, send_x, recv_x, send_s, recv_s,
):
    depth = r_hbm.shape[1]
    steps = depth // chunk
    shard = r_hbm.shape[0] // regions
    parts = regions * frames // 384
    me = lax.axis_index("qry")
    chip = me // 2
    core = me % 2
    sibling = chip * 2 + (1 - core)
    right = ((chip + 1) % chips) * 2 + core
    left = ((chip + chips - 1) % chips) * 2 + core

    def cols(c):
        return pl.ds(pl.multiple_of(c * chunk, 128), chunk)

    def own_copy(c):
        return pltpu.make_async_copy(
            r_hbm.at[:, cols(c)], r_buf.at[0, :, cols(c)], own_sem.at[c]
        )

    def q_copy(c):
        return pltpu.make_async_copy(q_hbm.at[:, cols(c)], q_buf.at[:, cols(c)], q_sem.at[c])

    def to_right(step, c):
        source = r_hbm if step == 0 else r_buf.at[2 * step]
        return pltpu.make_async_remote_copy(
            src_ref=source.at[:, cols(c)],
            dst_ref=r_buf.at[2 * step + 2, :, cols(c)],
            send_sem=send_x.at[step, c],
            recv_sem=recv_x.at[step, c],
            device_id={"qry": right},
            device_id_type=MESH,
        )

    def to_sibling(step, c):
        source = r_hbm if step == 0 else r_buf.at[2 * step]
        return pltpu.make_async_remote_copy(
            src_ref=source.at[:, cols(c)],
            dst_ref=r_buf.at[2 * step + 1, :, cols(c)],
            send_sem=send_s.at[step, c],
            recv_sem=recv_s.at[step, c],
            device_id={"qry": sibling},
            device_id_type=MESH,
        )

    def start_own(c, carry):
        own_copy(c).start()
        q_copy(c).start()
        return carry

    lax.fori_loop(0, steps, start_own, 0)
    barrier = pltpu.get_barrier_semaphore()
    greet = (sibling, right) if chips == 2 else (sibling, right, left)
    for device in greet:
        pl.semaphore_signal(barrier, inc=1, device_id={"qry": device}, device_id_type=MESH)
    pl.semaphore_wait(barrier, len(greet))

    def start_sends(c, carry):
        to_right(0, c).start()
        to_sibling(0, c).start()
        return carry

    lax.fori_loop(0, steps, start_sends, 0)

    def multiply(slot, side, c):
        block = r_buf[slot, :, cols(c)]

        def one_part(i, carry):
            rows = pl.ds(pl.multiple_of(i * 384, 128), 384)
            term = lax.dot_general(
                block, q_buf[rows, cols(c)], (((1,), (1,)), ((), ())),
                preferred_element_type=jnp.float32,
            )
            kept = acc[side, i]
            acc[side, i] = jnp.where(c == 0, term, kept + term)
            return carry

        lax.fori_loop(0, parts, one_part, 0)

    def finish(step, side):
        origin = (chip + chips - step) % chips
        source = origin * 2 + (core if side == 0 else 1 - core)
        total = jnp.zeros((shard, frames), jnp.float32)
        for i in range(parts):
            best = jnp.max(acc[side, i].reshape(regions, shard, 384), axis=0)
            for k in range(384 // frames):
                total = total + best[:, k * frames : (k + 1) * frames]
        out_ref[source] = total * scale

    acc[...] = jnp.zeros_like(acc)

    def first_own(c, carry):
        own_copy(c).wait()
        q_copy(c).wait()
        multiply(0, 0, c)
        return carry

    lax.fori_loop(0, steps, first_own, 0)
    finish(0, 0)

    def first_sibling(c, carry):
        to_sibling(0, c).wait_recv()
        multiply(1, 1, c)
        return carry

    lax.fori_loop(0, steps, first_sibling, 0)
    finish(0, 1)
    for step in range(1, chips):

        def later(c, carry):
            to_right(step - 1, c).wait_recv()
            to_sibling(step, c).start()
            if step < chips - 1:
                to_right(step, c).start()
            multiply(2 * step, 0, c)
            to_sibling(step, c).wait_recv()
            multiply(2 * step + 1, 1, c)
            return carry

        lax.fori_loop(0, steps, later, 0)
        finish(step, 0)
        finish(step, 1)

    def drain(c, carry):
        for step in range(chips):
            to_sibling(step, c).wait_send()
            if step < chips - 1:
                to_right(step, c).wait_send()
        return carry

    lax.fori_loop(0, steps, drain, 0)


def frame_sims(query_mat, ref_mat, regions, senders):
    depth = query_mat.shape[1]
    frames = query_mat.shape[0] // regions
    rows = ref_mat.shape[0]
    shard = rows // regions
    chips = senders // 2
    chunk = 768 if depth % 768 == 0 else depth
    steps = depth // chunk
    parts = regions * frames // 384
    scale = 1.0 / (regions * math.sqrt(depth))
    return pl.pallas_call(
        functools.partial(sims_kernel, chips, regions, frames, scale, chunk),
        out_shape=jax.ShapeDtypeStruct((senders, shard, frames), jnp.float32),
        in_specs=[pl.BlockSpec(memory_space=pl.ANY)] * 2,
        out_specs=pl.BlockSpec(memory_space=pltpu.VMEM),
        scratch_shapes=[
            pltpu.VMEM(query_mat.shape, jnp.bfloat16),
            pltpu.VMEM((senders, rows, depth), jnp.bfloat16),
            pltpu.VMEM((2, parts, rows, 384), jnp.float32),
            pltpu.SemaphoreType.DMA((steps,)),
            pltpu.SemaphoreType.DMA((steps,)),
            pltpu.SemaphoreType.DMA((chips, steps)),
            pltpu.SemaphoreType.DMA((chips, steps)),
            pltpu.SemaphoreType.DMA((chips, steps)),
            pltpu.SemaphoreType.DMA((chips, steps)),
        ],
        compiler_params=pltpu.CompilerParams(
            collective_id=0, has_side_effects=True, vmem_limit_bytes=48 << 20
        ),
        name="frame_sims",
    )(query_mat, ref_mat)


def net_kernel(
    tiles_p, tiles_f, where_ref, map_ref, w1_ref, b1_ref, w2_ref, b2_ref, w3_ref, b3_ref,
    w4_ref, out_ref, z_buf, x_buf, first_buf, second_buf, w2_full, w3_full,
):
    side = tiles_p + 4
    rows = side * PITCH
    wide = map_ref.shape[0]
    lane = lax.broadcasted_iota(jnp.int32, (1, 128), 1)
    low_a = lane < 64
    low_b = (lane % 64) < 32

    w2_full[...] = jnp.zeros_like(w2_full)
    taps = {(0, 0): 0, (0, 1): 1, (1, 0): 2, (1, 1): -1}
    for g in range(2):
        for h in range(2):
            for a in range(2):
                for b in range(2):
                    row = ((g * 2 + h) * 4 + a * 2 + b) * 32
                    for u in range(2):
                        for v in range(2):
                            di = taps[g, a] - u + 1
                            dj = taps[h, b] - v + 1
                            if 0 <= di < 3 and 0 <= dj < 3:
                                col = u * 128 + v * 64
                                w2_full[row : row + 32, col : col + 64] = w2_ref[di * 3 + dj]
    for k in range(9):
        w3_full[k * 64 : (k + 1) * 64, :] = w3_ref[k]
    w3_full[576:640, :] = jnp.zeros((64, 128), jnp.bfloat16)

    source = lax.broadcasted_iota(jnp.int32, (wide, 128), 0)
    target = lax.broadcasted_iota(jnp.int32, (wide, 128), 1)
    whole = map_ref[...]
    high = whole.astype(jnp.bfloat16)
    lower = (whole - high.astype(jnp.float32)).astype(jnp.bfloat16)
    z_buf[...] = jnp.zeros_like(z_buf)
    for rr in range(6):
        pick = jnp.where(source == 4 * target - 1 + rr, 1.0, 0.0).astype(jnp.bfloat16)
        for part, value in enumerate((high, lower)):
            z_buf[part, 8 : 8 + wide, rr * 128 : (rr + 1) * 128] = jnp.dot(
                value, pick, preferred_element_type=jnp.float32
            )
    for block in range(side):
        pieces = []
        for part in (0, 1, 0):
            for rr in range(6):
                pieces.append(
                    z_buf[part, 4 * block + 7 : 4 * block + 15, rr * 128 : (rr + 1) * 128]
                )
        flat = jnp.concatenate(pieces, axis=0)
        x_buf[block * PITCH : (block + 1) * PITCH, :] = jnp.transpose(flat)[:PITCH]

    shape = (side, PITCH, 128)
    at_f = lax.broadcasted_iota(jnp.int32, shape, 0) + (where_ref[1] - 2)
    at_p = lax.broadcasted_iota(jnp.int32, shape, 1) + (where_ref[0] - 2)
    inside = (at_f >= 0) & (at_f < where_ref[3]) & (at_p >= 0) & (at_p < where_ref[2])
    inside = jnp.where(inside, 1.0, 0.0).reshape(rows, 128)

    made = jnp.dot(
        x_buf[...].astype(jnp.bfloat16), w1_ref[...], preferred_element_type=jnp.float32
    )
    best = jnp.maximum(
        jnp.maximum(made[:, 0:128], made[:, 128:256]),
        jnp.maximum(made[:, 256:384], made[:, 384:512]),
    )
    first = jnp.maximum(best + b1_ref[...], 0.0)
    first = jnp.where(inside > 0.5, first, 0.0).astype(jnp.bfloat16).astype(jnp.float32)
    first_buf[0:LEAD, :] = jnp.zeros((LEAD, 128), jnp.float32)
    first_buf[LEAD + rows :, :] = jnp.zeros((LEAD, 128), jnp.float32)
    first_buf[LEAD : LEAD + rows, :] = first

    start = LEAD - PITCH
    more = rows + 2 * PITCH
    shifted = jnp.where(
        low_a, first_buf[start + 1 : start + 1 + more, :], first_buf[start - 1 : start - 1 + more, :]
    )
    across = jnp.where(
        low_b, first_buf[LEAD + PITCH : LEAD + PITCH + rows, :], first_buf[start : start + rows, :]
    )
    both = jnp.where(low_b, shifted[2 * PITCH :], shifted[:rows])
    stacked = jnp.concatenate(
        [first, across, shifted[PITCH : PITCH + rows], both], axis=1
    ).astype(jnp.bfloat16)
    made = jnp.dot(stacked, w2_full[...], preferred_element_type=jnp.float32)
    best = jnp.maximum(made[:, 0:128], made[:, 128:256])
    best = jnp.maximum(best, pltpu.roll(best, 64, 1))
    second = jnp.maximum(best + b2_ref[...], 0.0)
    second = jnp.where(inside > 0.5, second, 0.0).astype(jnp.bfloat16).astype(jnp.float32)
    second_buf[0:LEAD, :] = jnp.zeros((LEAD, 128), jnp.float32)
    second_buf[LEAD + rows :, :] = jnp.zeros((LEAD, 128), jnp.float32)
    second_buf[LEAD : LEAD + rows, :] = second

    def moved(k):
        di, dj = k // 3, k % 3
        begin = LEAD + (dj - 1) * PITCH + di - 1
        return second_buf[begin : begin + rows, :]

    groups = []
    for k in range(0, 9, 2):
        groups.append(jnp.where(low_a, moved(k), moved(k + 1)) if k < 8 else moved(k))
    stacked = jnp.concatenate(groups, axis=1).astype(jnp.bfloat16)
    made = jnp.dot(stacked, w3_full[...], preferred_element_type=jnp.float32)
    third = jnp.maximum(made + b3_ref[...], 0.0).astype(jnp.bfloat16).astype(jnp.float32)
    weighted = third * w4_ref[...]
    out_ref[...] = jnp.sum(weighted.reshape(side, PITCH, 128), axis=2)


def first_matrix(weight):
    outputs = weight.shape[2]
    table = np.zeros((6, 8, 2, 2, 2, 2, 9), np.float32)
    for a in range(2):
        for b in range(2):
            for u in range(2):
                for v in range(2):
                    for di in range(3):
                        for dj in range(3):
                            table[2 * a + u + di, 2 * b + v + dj, u, v, a, b, di * 3 + dj] = 1.0
    full = jnp.dot(
        table.reshape(48 * 16, 9), weight.reshape(9, outputs), precision=lax.Precision.HIGHEST
    ).reshape(48, 16 * outputs)
    high = lax.reduce_precision(full, 8, 7)
    return jnp.concatenate([high, high, full - high], axis=0).astype(jnp.bfloat16)


def network(
    wide_map, where, tiles, w1, b1, w2, b2, w3, b3, w4
):
    side = tiles + 4
    rows = side * PITCH
    vmem = pl.BlockSpec(memory_space=pltpu.VMEM)
    return pl.pallas_call(
        functools.partial(net_kernel, tiles, tiles),
        out_shape=jax.ShapeDtypeStruct((side, PITCH), jnp.float32),
        in_specs=[pl.BlockSpec(memory_space=pltpu.SMEM)] + [vmem] * 8,
        out_specs=vmem,
        scratch_shapes=[
            pltpu.VMEM((2, wide_map.shape[0] + 16, 768), jnp.float32),
            pltpu.VMEM((rows, 144), jnp.float32),
            pltpu.VMEM((rows + 2 * LEAD, 128), jnp.float32),
            pltpu.VMEM((rows + 2 * LEAD, 128), jnp.float32),
            pltpu.VMEM((512, 256), jnp.bfloat16),
            pltpu.VMEM((640, 128), jnp.bfloat16),
        ],
        compiler_params=pltpu.CompilerParams(vmem_limit_bytes=48 << 20),
        name="network",
    )(
        where,
        wide_map,
        w1,
        jnp.tile(b1, 4)[None],
        jnp.transpose(w2, (0, 1, 3, 2)).reshape(9, w2.shape[3], w2.shape[2]),
        jnp.tile(b2, 2)[None],
        jnp.transpose(w3, (0, 1, 3, 2)).reshape(9, w3.shape[3], w3.shape[2]),
        b3[None],
        w4.astype(jnp.float32)[None],
    )


def padded(block, sides, width):
    for axis, dim in sides:
        count = lax.axis_size(axis)
        forward = [(i, i + 1) for i in range(count - 1)]
        backward = [(target, source) for source, target in forward]
        low = lax.ppermute(
            lax.slice_in_dim(block, block.shape[dim] - width, None, axis=dim), axis, forward
        )
        high = lax.ppermute(lax.slice_in_dim(block, 0, width, axis=dim), axis, backward)
        block = jnp.concatenate([low, block, high], axis=dim)
    return block


def body(
    query_feats, ref_feats, pair_table, lengths, query_len, conv1_weight, conv1_bias,
    conv2_weight, conv2_bias, conv3_weight, conv3_bias, conv4_weight, conv4_bias,
):
    qry_index = lax.axis_index("qry")
    ref_index = lax.axis_index("ref")
    senders = lax.axis_size("qry")
    frames, regions, channels = query_feats.shape
    query_mat = jnp.transpose(query_feats, (1, 0, 2)).reshape(regions * frames, channels)
    ref_mat = jnp.transpose(ref_feats, (1, 2, 0, 3)).reshape(-1, channels)
    sims = frame_sims(query_mat, ref_mat, regions, senders)
    active = lax.dynamic_slice(pair_table, (qry_index, ref_index), (1, 1)) == 1
    sims = jnp.transpose(sims, (1, 0, 2)).reshape(frames, frames)
    sims = jnp.where(active, sims, 0.0)
    wide_map = padded(sims, (("ref", 0), ("qry", 1)), HALO)
    tiles = frames // 4
    where = jnp.stack(
        [
            qry_index * tiles,
            ref_index * tiles,
            jnp.int32(senders * tiles),
            jnp.int32(lax.axis_size("ref") * tiles),
        ]
    ).astype(jnp.int32)
    scores = network(
        wide_map, where, tiles, first_matrix(conv1_weight), conv1_bias, conv2_weight,
        conv2_bias, conv3_weight, conv3_bias, conv4_weight,
    )
    score_map = jnp.transpose(scores[2 : 2 + tiles, 2 : 2 + tiles]) + conv4_bias[0]
    ends = jnp.cumsum(lengths)
    starts = ends - lengths
    column = ref_index * tiles + jnp.arange(tiles, dtype=jnp.int32)
    member = (column[:, None] >= starts[None, :]) & (column[:, None] < ends[None, :])
    peaks = jnp.max(jnp.where(member[None], score_map[:, :, None], -jnp.inf), axis=1)
    peaks = lax.pmax(peaks, "ref")
    row_ids = qry_index * tiles + jnp.arange(tiles, dtype=jnp.int32)
    partial_value = jnp.sum(jnp.where((row_ids < query_len[0])[:, None], peaks, 0.0), axis=0)
    totals = lax.psum(partial_value, "qry")
    return (score_map, totals / query_len[0].astype(jnp.float32))


def solution(mesh):
    placed = (
        P(("groups", "qry"), None, None),
        P(("groups", "ref"), "qry", None, None),
        P("groups", None),
        P("groups"),
        P("groups"),
    ) + (P(),) * 8
    return jax.shard_map(
        body,
        mesh=mesh,
        in_specs=placed,
        out_specs=(P(("groups", "qry"), "ref"), P("groups")),
        check_vma=False,
    )
```

```python
import functools
import math

import jax
import jax.numpy as jnp
import numpy as np
from jax import lax
from jax.experimental import pallas as pl
from jax.experimental.pallas import tpu as pltpu
from jax.sharding import PartitionSpec as P

MESH = pl.DeviceIdType.MESH
HALO = 8
PITCH = 40
LEAD = 48


def whole_kernel(
    chips, others, regions, frames, scale, chunk, pair_ref, lengths_ref, len_ref, b4_ref,
    w1_ref, b1_ref, w2_ref, b2_ref, w3_ref, b3_ref, w4_ref, q_hbm, r_hbm,
    scores_ref, totals_ref,
    q_buf, r_buf, acc, sims_buf, map_buf, z_buf, x_buf, first_buf, second_buf, w2_full, w3_full,
    peaks_buf, sums_buf,
    q_sem, own_sem, send_x, recv_x, send_s, recv_s, send_h, recv_h, send_p, recv_p, send_t, recv_t,
):
    depth = r_hbm.shape[1]
    steps = depth // chunk
    shard = r_hbm.shape[0] // regions
    parts = regions * frames // 384
    me = lax.axis_index("qry")
    chip = me // 2
    core = me % 2
    sibling = chip * 2 + (1 - core)
    right = ((chip + 1) % chips) * 2 + core
    senders = 2 * chips
    col = lax.axis_index("ref")

    def reachable(move_q, move_r):
        fits = (me + move_q >= 0) & (me + move_q < senders)
        return fits & (col + move_r >= 0) & (col + move_r < others)

    def cols(c):
        return pl.ds(pl.multiple_of(c * chunk, 128), chunk)

    def own_copy(c):
        return pltpu.make_async_copy(
            r_hbm.at[:, cols(c)], r_buf.at[0, :, cols(c)], own_sem.at[c]
        )

    def q_copy(c):
        return pltpu.make_async_copy(q_hbm.at[:, cols(c)], q_buf.at[:, cols(c)], q_sem.at[c])

    def to_right(step, c):
        source = r_hbm if step == 0 else r_buf.at[2 * step]
        return pltpu.make_async_remote_copy(
            src_ref=source.at[:, cols(c)],
            dst_ref=r_buf.at[2 * step + 2, :, cols(c)],
            send_sem=send_x.at[step, c],
            recv_sem=recv_x.at[step, c],
            device_id={"qry": right},
            device_id_type=MESH,
        )

    def to_sibling(step, c):
        source = r_hbm if step == 0 else r_buf.at[2 * step]
        return pltpu.make_async_remote_copy(
            src_ref=source.at[:, cols(c)],
            dst_ref=r_buf.at[2 * step + 1, :, cols(c)],
            send_sem=send_s.at[step, c],
            recv_sem=recv_s.at[step, c],
            device_id={"qry": sibling},
            device_id_type=MESH,
        )

    def start_own(c, carry):
        own_copy(c).start()
        q_copy(c).start()
        return carry

    lax.fori_loop(0, steps, start_own, 0)
    map_buf[...] = jnp.zeros_like(map_buf)
    barrier = pltpu.get_barrier_semaphore()
    for k in range(1, senders):
        device = {"qry": (me + k) % senders}
        pl.semaphore_signal(barrier, inc=1, device_id=device, device_id_type=MESH)
    for k in range(1, others):
        device = {"ref": (col + k) % others}
        pl.semaphore_signal(barrier, inc=1, device_id=device, device_id_type=MESH)
    for move_q in (1, senders - 1):
        for move_r in (1, others - 1):
            device = {"qry": (me + move_q) % senders, "ref": (col + move_r) % others}
            pl.semaphore_signal(barrier, inc=1, device_id=device, device_id_type=MESH)
    pl.semaphore_wait(barrier, senders - 1 + others - 1 + 4)

    def start_sends(c, carry):
        to_right(0, c).start()
        to_sibling(0, c).start()
        return carry

    lax.fori_loop(0, steps, start_sends, 0)

    def multiply(slot, side, c):
        block = r_buf[slot, :, cols(c)]

        def one_part(i, carry):
            rows = pl.ds(pl.multiple_of(i * 384, 128), 384)
            term = lax.dot_general(
                block, q_buf[rows, cols(c)], (((1,), (1,)), ((), ())),
                preferred_element_type=jnp.float32,
            )
            kept = acc[side, i]
            acc[side, i] = jnp.where(c == 0, term, kept + term)
            return carry

        lax.fori_loop(0, parts, one_part, 0)

    def finish(step, side):
        origin = (chip + chips - step) % chips
        source = origin * 2 + (core if side == 0 else 1 - core)
        total = jnp.zeros((shard, frames), jnp.float32)
        for i in range(parts):
            best = jnp.max(acc[side, i].reshape(regions, shard, 384), axis=0)
            for k in range(384 // frames):
                total = total + best[:, k * frames : (k + 1) * frames]
        sims_buf[source] = total * (scale * active)

    active = pair_ref[me, col].astype(jnp.float32)
    acc[...] = jnp.zeros_like(acc)
    build_weights(w2_ref, w3_ref, w2_full, w3_full)

    def first_own(c, carry):
        own_copy(c).wait()
        q_copy(c).wait()
        multiply(0, 0, c)
        return carry

    lax.fori_loop(0, steps, first_own, 0)
    finish(0, 0)

    def first_sibling(c, carry):
        to_sibling(0, c).wait_recv()
        multiply(1, 1, c)
        return carry

    lax.fori_loop(0, steps, first_sibling, 0)
    finish(0, 1)
    for step in range(1, chips):

        def later(c, carry):
            to_right(step - 1, c).wait_recv()
            to_sibling(step, c).start()
            if step < chips - 1:
                to_right(step, c).start()
            multiply(2 * step, 0, c)
            to_sibling(step, c).wait_recv()
            multiply(2 * step + 1, 1, c)
            return carry

        lax.fori_loop(0, steps, later, 0)
        finish(step, 0)
        finish(step, 1)

    def drain(c, carry):
        for step in range(chips):
            to_sibling(step, c).wait_send()
            if step < chips - 1:
                to_right(step, c).wait_send()
        return carry

    lax.fori_loop(0, steps, drain, 0)

    for b in range(senders):
        map_buf.at[1][pl.ds(HALO + b, shard, stride=senders), :] = sims_buf[b]

    def halo_copy(k, move_q, move_r):
        if move_r == 0:
            source, target = pl.ds(HALO, frames), pl.ds(HALO, frames)
        elif move_r == 1:
            source, target = pl.ds(frames, HALO), pl.ds(0, HALO)
        else:
            source, target = pl.ds(HALO, HALO), pl.ds(HALO + frames, HALO)
        return pltpu.make_async_remote_copy(
            src_ref=map_buf.at[1, source],
            dst_ref=map_buf.at[1 - move_q, target],
            send_sem=send_h.at[k],
            recv_sem=recv_h.at[k],
            device_id={"qry": me + move_q, "ref": col + move_r},
            device_id_type=MESH,
        )

    moves = [(q, r) for q in (-1, 1, 0) for r in (-1, 1, 0) if (q, r) != (0, 0)]
    for k, (move_q, move_r) in enumerate(moves):

        @pl.when(reachable(move_q, move_r))
        def _():
            halo_copy(k, move_q, move_r).start()

    for k, (move_q, move_r) in enumerate(moves):

        @pl.when(reachable(-move_q, -move_r))
        def _():
            halo_copy(k, move_q, move_r).wait_recv()

    for k, (move_q, move_r) in enumerate(moves):

        @pl.when(reachable(move_q, move_r))
        def _():
            halo_copy(k, move_q, move_r).wait_send()

    tiles = frames // 4
    scores = network(
        tiles, (me * tiles, col * tiles, senders * tiles, others * tiles), map_buf, w1_ref, b1_ref,
        b2_ref, b3_ref, w4_ref, z_buf, x_buf, first_buf, second_buf, w2_full, w3_full,
    ) + b4_ref[0]
    scores_ref[...] = scores
    slot_f = lax.broadcasted_iota(jnp.int32, scores.shape, 0)
    column = slot_f + (col * tiles - 2)
    own = (slot_f >= 2) & (slot_f < 2 + tiles)
    peaks_buf[0] = jnp.zeros_like(peaks_buf[0])
    begin = jnp.int32(0)
    for v in range(lengths_ref.shape[0]):
        end = begin + lengths_ref[v]
        member = own & (column >= begin) & (column < end)
        peaks_buf[0, v : v + 1, :PITCH] = jnp.max(
            jnp.where(member, scores, -jnp.inf), axis=0, keepdims=True
        )
        begin = end

    def peak_copy(k):
        return pltpu.make_async_remote_copy(
            src_ref=peaks_buf.at[0],
            dst_ref=peaks_buf.at[k],
            send_sem=send_p.at[k],
            recv_sem=recv_p.at[k],
            device_id={"ref": (col + k) % others},
            device_id_type=MESH,
        )

    def sum_copy(k):
        return pltpu.make_async_remote_copy(
            src_ref=sums_buf.at[0],
            dst_ref=sums_buf.at[k],
            send_sem=send_t.at[k],
            recv_sem=recv_t.at[k],
            device_id={"qry": (me + k) % senders},
            device_id_type=MESH,
        )

    for k in range(1, others):
        peak_copy(k).start()
    for k in range(1, others):
        peak_copy(k).wait_recv()
    peaks = jnp.max(peaks_buf[...], axis=0)
    lane = lax.broadcasted_iota(jnp.int32, peaks.shape, 1)
    counted = (lane >= 2) & (lane < 2 + tiles) & (lane + (me * tiles - 2) < len_ref[0])
    partial_sum = jnp.sum(jnp.where(counted, peaks, 0.0), axis=1, keepdims=True)
    sums_buf[0] = jnp.broadcast_to(partial_sum, peaks.shape)
    for k in range(1, senders):
        sum_copy(k).start()
    for k in range(1, senders):
        sum_copy(k).wait_recv()
    totals_ref[...] = jnp.sum(sums_buf[...], axis=0) / len_ref[0].astype(jnp.float32)
    for k in range(1, others):
        peak_copy(k).wait_send()
    for k in range(1, senders):
        sum_copy(k).wait_send()


def build_weights(w2_ref, w3_ref, w2_full, w3_full):
    w2_full[...] = jnp.zeros_like(w2_full)
    taps = {(0, 0): 0, (0, 1): 1, (1, 0): 2, (1, 1): -1}
    for g in range(2):
        for h in range(2):
            for a in range(2):
                for b in range(2):
                    row = ((g * 2 + h) * 4 + a * 2 + b) * 32
                    for u in range(2):
                        for v in range(2):
                            di = taps[g, a] - u + 1
                            dj = taps[h, b] - v + 1
                            if 0 <= di < 3 and 0 <= dj < 3:
                                col = u * 128 + v * 64
                                w2_full[row : row + 32, col : col + 64] = w2_ref[di * 3 + dj]
    for k in range(9):
        w3_full[k * 64 : (k + 1) * 64, :] = w3_ref[k]
    w3_full[576:640, :] = jnp.zeros((64, 128), jnp.bfloat16)


def network(
    tiles, where_ref, map_ref, w1_ref, b1_ref, b2_ref, b3_ref, w4_ref,
    z_buf, x_buf, first_buf, second_buf, w2_full, w3_full,
):
    side = tiles + 4
    rows = side * PITCH
    wide = map_ref.shape[1]
    frames = map_ref.shape[2]
    lane = lax.broadcasted_iota(jnp.int32, (1, 128), 1)
    low_a = lane < 64
    low_b = (lane % 64) < 32

    source = lax.broadcasted_iota(jnp.int32, (3 * frames, 128), 0)
    target = lax.broadcasted_iota(jnp.int32, (3 * frames, 128), 1)
    whole = jnp.concatenate([map_ref[0], map_ref[1], map_ref[2]], axis=1)
    high = whole.astype(jnp.bfloat16)
    lower = (whole - high.astype(jnp.float32)).astype(jnp.bfloat16)
    z_buf[...] = jnp.zeros_like(z_buf)
    for rr in range(6):
        pick = jnp.where(source == 4 * target + (frames - 9) + rr, 1.0, 0.0).astype(jnp.bfloat16)
        for part, value in enumerate((high, lower)):
            z_buf[part, 8 : 8 + wide, rr * 128 : (rr + 1) * 128] = jnp.dot(
                value, pick, preferred_element_type=jnp.float32
            )
    for block in range(side):
        pieces = []
        for part in (0, 1, 0):
            for rr in range(6):
                pieces.append(
                    z_buf[part, 4 * block + 7 : 4 * block + 15, rr * 128 : (rr + 1) * 128]
                )
        flat = jnp.concatenate(pieces, axis=0)
        x_buf[block * PITCH : (block + 1) * PITCH, :] = jnp.transpose(flat)[:PITCH]

    shape = (side, PITCH, 128)
    at_f = lax.broadcasted_iota(jnp.int32, shape, 0) + (where_ref[1] - 2)
    at_p = lax.broadcasted_iota(jnp.int32, shape, 1) + (where_ref[0] - 2)
    inside = (at_f >= 0) & (at_f < where_ref[3]) & (at_p >= 0) & (at_p < where_ref[2])
    inside = jnp.where(inside, 1.0, 0.0).reshape(rows, 128)

    made = jnp.dot(
        x_buf[...].astype(jnp.bfloat16), w1_ref[...], preferred_element_type=jnp.float32
    )
    best = jnp.maximum(
        jnp.maximum(made[:, 0:128], made[:, 128:256]),
        jnp.maximum(made[:, 256:384], made[:, 384:512]),
    )
    first = jnp.maximum(best + b1_ref[...], 0.0)
    first = jnp.where(inside > 0.5, first, 0.0).astype(jnp.bfloat16).astype(jnp.float32)
    first_buf[0:LEAD, :] = jnp.zeros((LEAD, 128), jnp.float32)
    first_buf[LEAD + rows :, :] = jnp.zeros((LEAD, 128), jnp.float32)
    first_buf[LEAD : LEAD + rows, :] = first

    start = LEAD - PITCH
    more = rows + 2 * PITCH
    shifted = jnp.where(
        low_a, first_buf[start + 1 : start + 1 + more, :], first_buf[start - 1 : start - 1 + more, :]
    )
    across = jnp.where(
        low_b, first_buf[LEAD + PITCH : LEAD + PITCH + rows, :], first_buf[start : start + rows, :]
    )
    both = jnp.where(low_b, shifted[2 * PITCH :], shifted[:rows])
    stacked = jnp.concatenate(
        [first, across, shifted[PITCH : PITCH + rows], both], axis=1
    ).astype(jnp.bfloat16)
    made = jnp.dot(stacked, w2_full[...], preferred_element_type=jnp.float32)
    best = jnp.maximum(made[:, 0:128], made[:, 128:256])
    best = jnp.maximum(best, pltpu.roll(best, 64, 1))
    second = jnp.maximum(best + b2_ref[...], 0.0)
    second = jnp.where(inside > 0.5, second, 0.0).astype(jnp.bfloat16).astype(jnp.float32)
    second_buf[0:LEAD, :] = jnp.zeros((LEAD, 128), jnp.float32)
    second_buf[LEAD + rows :, :] = jnp.zeros((LEAD, 128), jnp.float32)
    second_buf[LEAD : LEAD + rows, :] = second

    def moved(k):
        di, dj = k // 3, k % 3
        begin = LEAD + (dj - 1) * PITCH + di - 1
        return second_buf[begin : begin + rows, :]

    groups = []
    for k in range(0, 9, 2):
        groups.append(jnp.where(low_a, moved(k), moved(k + 1)) if k < 8 else moved(k))
    stacked = jnp.concatenate(groups, axis=1).astype(jnp.bfloat16)
    made = jnp.dot(stacked, w3_full[...], preferred_element_type=jnp.float32)
    third = jnp.maximum(made + b3_ref[...], 0.0).astype(jnp.bfloat16).astype(jnp.float32)
    weighted = third * w4_ref[...]
    return jnp.sum(weighted.reshape(side, PITCH, 128), axis=2)


def first_matrix(weight):
    outputs = weight.shape[2]
    table = np.zeros((6, 8, 2, 2, 2, 2, 9), np.float32)
    for a in range(2):
        for b in range(2):
            for u in range(2):
                for v in range(2):
                    for di in range(3):
                        for dj in range(3):
                            table[2 * a + u + di, 2 * b + v + dj, u, v, a, b, di * 3 + dj] = 1.0
    full = jnp.dot(
        table.reshape(48 * 16, 9), weight.reshape(9, outputs), precision=lax.Precision.HIGHEST
    ).reshape(48, 16 * outputs)
    high = lax.reduce_precision(full, 8, 7)
    return jnp.concatenate([high, high, full - high], axis=0).astype(jnp.bfloat16)


def body(
    query_feats, ref_feats, pair_table, lengths, query_len, conv1_weight, conv1_bias,
    conv2_weight, conv2_bias, conv3_weight, conv3_bias, conv4_weight, conv4_bias,
):
    senders = lax.axis_size("qry")
    others = lax.axis_size("ref")
    frames, regions, depth = query_feats.shape
    query_mat = jnp.transpose(query_feats, (1, 0, 2)).reshape(regions * frames, depth)
    ref_mat = jnp.transpose(ref_feats, (1, 2, 0, 3)).reshape(-1, depth)
    videos = lengths.shape[0]
    video_rows = -(-videos // 8) * 8
    shard_rows = ref_mat.shape[0]
    chips = senders // 2
    chunk = 256 if depth % 256 == 0 else depth
    steps = depth // chunk
    parts = regions * frames // 384
    tiles = frames // 4
    side = tiles + 4
    rows = side * PITCH
    scale = 1.0 / (regions * math.sqrt(depth))
    vmem = pl.BlockSpec(memory_space=pltpu.VMEM)
    smem = pl.BlockSpec(memory_space=pltpu.SMEM)
    hbm = pl.BlockSpec(memory_space=pl.ANY)
    dma = pltpu.SemaphoreType.DMA
    scores, totals = pl.pallas_call(
        functools.partial(whole_kernel, chips, others, regions, frames, scale, chunk),
        out_shape=(
            jax.ShapeDtypeStruct((side, PITCH), jnp.float32),
            jax.ShapeDtypeStruct((video_rows, 128), jnp.float32),
        ),
        in_specs=[smem] * 4 + [vmem] * 7 + [hbm] * 2,
        out_specs=(vmem, vmem),
        scratch_shapes=[
            pltpu.VMEM(query_mat.shape, jnp.bfloat16),
            pltpu.VMEM((senders, shard_rows, depth), jnp.bfloat16),
            pltpu.VMEM((2, parts, shard_rows, 384), jnp.float32),
            pltpu.VMEM((senders, frames // senders, frames), jnp.float32),
            pltpu.VMEM((3, frames + 2 * HALO, frames), jnp.float32),
            pltpu.VMEM((2, frames + 4 * HALO, 768), jnp.float32),
            pltpu.VMEM((rows, 144), jnp.float32),
            pltpu.VMEM((rows + 2 * LEAD, 128), jnp.float32),
            pltpu.VMEM((rows + 2 * LEAD, 128), jnp.float32),
            pltpu.VMEM((512, 256), jnp.bfloat16),
            pltpu.VMEM((640, 128), jnp.bfloat16),
            pltpu.VMEM((others, video_rows, 128), jnp.float32),
            pltpu.VMEM((senders, video_rows, 128), jnp.float32),
            dma((steps,)),
            dma((steps,)),
            dma((chips, steps)),
            dma((chips, steps)),
            dma((chips, steps)),
            dma((chips, steps)),
            dma((8,)),
            dma((8,)),
            dma((others,)),
            dma((others,)),
            dma((senders,)),
            dma((senders,)),
        ],
        compiler_params=pltpu.CompilerParams(
            collective_id=0, has_side_effects=True, vmem_limit_bytes=56 << 20
        ),
        name="whole",
    )(
        pair_table,
        lengths,
        query_len,
        conv4_bias,
        first_matrix(conv1_weight),
        jnp.tile(conv1_bias, 4)[None],
        jnp.transpose(conv2_weight, (0, 1, 3, 2)).reshape(
            9, conv2_weight.shape[3], conv2_weight.shape[2]
        ),
        jnp.tile(conv2_bias, 2)[None],
        jnp.transpose(conv3_weight, (0, 1, 3, 2)).reshape(
            9, conv3_weight.shape[3], conv3_weight.shape[2]
        ),
        conv3_bias[None],
        conv4_weight.astype(jnp.float32)[None],
        query_mat,
        ref_mat,
    )
    score_map = jnp.transpose(scores[2 : 2 + tiles, 2 : 2 + tiles])
    return (score_map, totals[:videos, 0])


def solution(mesh):
    placed = (
        P(("groups", "qry"), None, None),
        P(("groups", "ref"), "qry", None, None),
        P("groups", None),
        P("groups"),
        P("groups"),
    ) + (P(),) * 8
    return jax.shard_map(
        body,
        mesh=mesh,
        in_specs=placed,
        out_specs=(P(("groups", "qry"), "ref"), P("groups")),
        check_vma=False,
    )
```
